32 devices in a mesh: groups: 2 (over x), row: 8 (over z, y), col: 2 (over core).
Axes of the slice: x: 2, y: 2, z: 4, core: 2. Of those that a mesh axis runs over, the one named last changes fastest.
Arguments:
- spectra: bfloat16 [4096, 16384], P(('groups', 'row', 'col')), parts along dimension 0, may hold values from -60 to 60
- block_order: int32 [4096], P('groups'), parts along dimension 0, may hold values from 0 to 2047, each once
- offsets: int32 [17], replicated, may hold values from -24 to 24, as said below
Outputs:
- similarity: float32 [4096, 2048], P(('groups', 'row', 'col')), parts along dimension 0
The draws below stay inside these ranges and needn't reach their ends.
There are 2 independent parts, one for each index of `groups`. The reference program is written for one: setup_inputs(seed, part) draws one part's arguments, and reference() takes and returns one part's arrays. A program takes and returns all parts, laid end to end along the dimension named above; an argument that names none is the same for every part. Nothing has to cross between parts.
Inputs may be any that keep to these rules, and one draw needn't show every extreme that they name: `offsets`: the 17 values are distinct, include 0 and 24, and the negative of each value is also among them.
All inputs are finite; a program needn't handle non-finite values.
Results may differ from the reference program's by a relative error of at most 0.0013.
Values may be sent and summed in bfloat16 or wider, within the bound.
A program may use at most 128 MiB of HBM per device.

```python
import math
import jax
import jax.numpy as jnp
from jax import lax

BINS = 16384
TAPS = 16
OFFS = 17
MAXOFF = 24
PADW = 64
NS = 2048


compound_total = 16


def draw_spectra(key, part):
    key_tmpl = jax.random.fold_in(key, 11)
    key_comp = jax.random.fold_in(key, 12)
    key_shift = jax.random.fold_in(key, 13)
    key_noise = jax.random.fold_in(key, 14)
    template = jnp.clip(jax.random.normal(key_tmpl, (compound_total, BINS), jnp.float32), -4.0, 4.0)
    compound = jax.random.randint(key_comp, (NS,), 0, compound_total)
    shift = jax.random.randint(key_shift, (NS,), -(MAXOFF // 2), MAXOFF // 2 + 1)
    where_bins = (jnp.arange(BINS)[None, :] - TAPS * shift[:, None]) % BINS
    clean = template[compound[:, None], where_bins]
    noise = jnp.clip(jax.random.normal(key_noise, (NS, BINS), jnp.float32), -4.0, 4.0)
    return (clean + 0.5 * noise).astype(jnp.bfloat16)


def draw_offsets(key, part):
    half_count = (OFFS - 1) // 2
    picked = jax.random.permutation(jax.random.fold_in(key, 21), MAXOFF - 1).astype(jnp.int32) + 1
    positive = jnp.concatenate([picked[:half_count - 1], jnp.full((1,), MAXOFF, jnp.int32)])
    values = jnp.concatenate([jnp.zeros((1,), jnp.int32), positive, -positive])
    placing = jax.random.permutation(jax.random.fold_in(key, 22), OFFS)
    return values[placing].astype(jnp.int32)


def setup_inputs(seed: int = 0, part: int = 0) -> dict:
    keys = jax.random.split(jax.random.key(seed), 4)
    part_splits = jax.random.split(jax.random.fold_in(keys[3], part), 4)
    return {
        "spectra": draw_spectra(jax.random.fold_in(jax.random.fold_in(keys[3], part), 71), part),
        "block_order": jax.random.permutation(part_splits[1], NS).astype(jnp.int32),
        "offsets": draw_offsets(jax.random.fold_in(keys[3], 71), part),
    }


def taps_table(count):
    steps = jnp.arange(count, dtype=jnp.float32)
    return (0.5 - 0.5 * jnp.cos(2.0 * math.pi * (steps + 0.5) / count)).astype(jnp.bfloat16)

def reference(spectra, block_order, offsets):
    total_rows, bins = spectra.shape
    coarse_len = bins // TAPS
    taps = taps_table(TAPS).astype(jnp.float32)
    coarse = jnp.einsum('idt,t->id', spectra.astype(jnp.float32).reshape(total_rows, coarse_len, TAPS), taps)
    scale = lax.rsqrt(lax.optimization_barrier(jnp.mean(coarse * coarse, axis=1, keepdims=True)) + 1e-06) * (1.0 / math.sqrt(coarse_len))
    unit = (coarse * scale).astype(jnp.bfloat16)
    ordered = jnp.take(unit, block_order, axis=0).astype(jnp.float32)
    padded = jnp.pad(ordered, ((0, 0), (PADW, PADW)))

    def one(best, offset):
        shifted = lax.dynamic_slice_in_dim(padded, PADW + offset, coarse_len, 1)
        scores = jnp.dot(ordered, shifted.T, precision=lax.Precision.HIGHEST, preferred_element_type=jnp.float32)
        return (jnp.maximum(best, scores), None)
    start = jnp.full((total_rows, total_rows), -1e+30, jnp.float32)
    best, unused = lax.scan(one, start, offsets)
    return best
```

```python
import functools
import math

import jax
import jax.numpy as jnp
import ml_dtypes
import numpy as np
from jax import lax
from jax.experimental import pallas as pl
from jax.experimental.pallas import tpu as pltpu
from jax.sharding import PartitionSpec as P

TAPS = 16
LANE = 128
WIN = 256
MESH = pl.DeviceIdType.MESH
UP, DOWN, ACROSS, SIB = range(4)


def decimation_weights():
    steps = np.arange(TAPS, dtype=np.float64)
    taps = (0.5 - 0.5 * np.cos(2.0 * math.pi * (steps + 0.5) / TAPS)).astype(ml_dtypes.bfloat16)
    full = np.kron(np.eye(LANE), taps.astype(np.float64)[:, None])
    return full.astype(ml_dtypes.bfloat16)


def kernel(cfg, off_ref, spec_ref, w_ref, bo_ref, out_ref,
           raw, coarse, buf, mine, stack, acc, perm, pick, hilo,
           in_sem, send_sem, recv_sem):
    nz, ny, nb, rows, feats, offs, keep_perm = cfg
    chunks = [(0, 3)] + [(t, min(2, feats // LANE - t)) for t in range(3, feats // LANE, 2)]
    nk = len(chunks)
    total = nb * rows
    tiles = total // WIN
    bins_part = TAPS * LANE

    row = lax.axis_index("row")
    core = lax.axis_index("col")
    z = row // ny
    y = row % ny
    me = row * 2 + core

    def block(zz, yy, cc):
        return (zz * ny + yy) * 2 + cc

    def target(way):
        if way == UP:
            return {"row": row + ny, "col": core}
        if way == DOWN:
            return {"row": row - ny, "col": core}
        if way == ACROSS:
            return {"row": z * ny + (1 - y), "col": core}
        return {"row": row, "col": 1 - core}

    def copy_of(k, blk, way):
        first, count = chunks[k]
        ref = buf.at[pl.ds(first, count), blk]
        return pltpu.make_async_remote_copy(
            src_ref=ref, dst_ref=ref,
            send_sem=send_sem.at[k, way, blk], recv_sem=recv_sem.at[k, blk],
            device_id=target(way), device_id_type=MESH)

    def arrived(k, blk):
        copy_of(k, blk, SIB).wait_recv()

    has_up = z < nz - 1
    has_down = z > 0

    loads = []
    for g in range(feats // LANE):
        load = pltpu.make_async_copy(
            spec_ref.at[:, pl.ds(g * bins_part, bins_part)], raw.at[g], in_sem.at[g])
        load.start()
        loads.append(load)

    barrier = pltpu.get_barrier_semaphore()

    def greet(way):
        pl.semaphore_signal(barrier, inc=1, device_id=target(way), device_id_type=MESH)

    greet(SIB)
    if ny == 2:
        greet(ACROSS)
    pl.when(has_up)(lambda: greet(UP))
    pl.when(has_down)(lambda: greet(DOWN))

    square = jnp.zeros((rows, 1), jnp.float32)
    pair = 2
    for g in range(0, feats // LANE, pair):
        for h in range(pair):
            loads[g + h].wait()
        x = jnp.concatenate([raw[g + h] for h in range(pair)], axis=0)
        c = jnp.dot(x, w_ref[...], preferred_element_type=jnp.float32)
        for h in range(pair):
            part = c[h * rows:(h + 1) * rows]
            coarse[g + h] = part
            square += jnp.sum(part * part, axis=1, keepdims=True)
    scale = lax.rsqrt(square * (1.0 / feats) + 1e-06) * (1.0 / math.sqrt(feats))
    for g in range(feats // LANE):
        buf[g, me] = (coarse[g] * scale).astype(jnp.bfloat16)

    pl.semaphore_wait(barrier, 1 + (1 if ny == 2 else 0)
                      + jnp.where(has_up, 1, 0) + jnp.where(has_down, 1, 0))

    def send_own(k):
        pl.when(has_up)(lambda: copy_of(k, me, UP).start())
        pl.when(has_down)(lambda: copy_of(k, me, DOWN).start())
        if ny == 2:
            copy_of(k, me, ACROSS).start()
        copy_of(k, me, SIB).start()

    def phase(k, t):
        if t < nz:
            @pl.when(z >= t)
            def _():
                blk = block(z - t, y, core)
                arrived(k, blk)
                pl.when(has_up)(lambda: copy_of(k, blk, UP).start())
                if ny == 2:
                    copy_of(k, blk, ACROSS).start()
                copy_of(k, blk, SIB).start()

            @pl.when(z + t < nz)
            def _():
                blk = block(z + t, y, core)
                arrived(k, blk)
                pl.when(has_down)(lambda: copy_of(k, blk, DOWN).start())
                if ny == 2:
                    copy_of(k, blk, ACROSS).start()
                copy_of(k, blk, SIB).start()
        if ny == 2:
            d = t - 1

            def across(blk):
                arrived(k, blk)
                copy_of(k, blk, SIB).start()

            pl.when(z >= d)(lambda: across(block(z - d, 1 - y, core)))
            if d > 0:
                pl.when(z + d < nz)(lambda: across(block(z + d, 1 - y, core)))

    def finish(k):
        for r in range(nb // 2):
            arrived(k, r * 2 + (1 - core))

    send_own(0)

    mine_pos = jnp.transpose(
        jnp.broadcast_to(bo_ref[pl.ds(me, 1), :].astype(jnp.float32), (LANE, LANE)))
    lane_ids = lax.broadcasted_iota(jnp.int32, (rows, LANE), 1).astype(jnp.float32)
    for b in range(nb):
        pick[:, b * LANE:(b + 1) * LANE] = jnp.where(
            mine_pos == lane_ids + float(b * LANE), 1.0, 0.0).astype(jnp.bfloat16)
    mine[:, :LANE] = jnp.zeros((rows, LANE), jnp.float32)
    mine[:, LANE + feats:] = jnp.zeros((rows, LANE), jnp.float32)

    def perm_tile(q):
        ids = lax.broadcasted_iota(jnp.int32, (total, LANE), 0)
        return jnp.where(ids == bo_ref[pl.ds(q, 1), :], 1.0, 0.0).astype(jnp.bfloat16)

    def build(q):
        perm[q] = perm_tile(q)

    for t in range(1, nz + 1):
        if keep_perm:
            per = -(-nb // nz)

            def fill(q, carry):
                build(q)
                return carry

            lax.fori_loop(min((t - 1) * per, nb), min(t * per, nb), fill, 0)
        if t == max(nz - 1, 1) and nk > 1:
            send_own(1)
        phase(0, t)
    finish(0)

    def window(k):
        first, count = chunks[k]
        got = jnp.concatenate(
            [buf[first + i].reshape(total, LANE) for i in range(count)], axis=1)
        mine[:, LANE * (1 + first):LANE * (1 + first + count)] = jnp.dot(
            pick[...], got, preferred_element_type=jnp.float32)
        span = mine[:, WIN * k:WIN * (k + 2)]
        for d in range(offs):
            shift = off_ref[d]
            shift = jnp.where(shift < 0, shift + 2 * WIN, shift)
            moved = pltpu.roll(span, shift, 1)
            stack[d * rows:(d + 1) * rows, :] = moved[:, LANE:LANE + WIN].astype(jnp.bfloat16)

        last = k == nk - 1

        def tile(i, carry):
            right = jnp.concatenate(
                [buf[2 * k + h, pl.ds(2 * i, 2)].reshape(WIN, LANE) for h in range(2)], axis=1)
            s = lax.dot_general(stack[...], right, (((1,), (1,)), ((), ())),
                                preferred_element_type=jnp.float32)
            if k == 0:
                acc[i] = s
            elif not last:
                acc[i] = acc[i] + s
            else:
                best = None
                for d in range(offs):
                    v = acc[i, d * rows:(d + 1) * rows] + s[d * rows:(d + 1) * rows]
                    best = v if best is None else jnp.maximum(best, v)
                high = best.astype(jnp.bfloat16)
                low = (best - high.astype(jnp.float32)).astype(jnp.bfloat16)
                hilo[i] = jnp.concatenate([high, low], axis=0)
            if not last:
                for t in range(1, nz + 1):
                    @pl.when(i == (t - 1) * tiles // nz)
                    def _():
                        if t == max(nz - 1, 1) and k + 2 < nk:
                            send_own(k + 2)
                        phase(k + 1, t)
            return carry

        lax.fori_loop(0, tiles, tile, 0)
        if not last:
            finish(k + 1)

    for k in range(nk):
        window(k)

    def order(q, carry):
        if keep_perm:
            right = jnp.concatenate([perm[2 * q], perm[2 * q + 1]], axis=1)
        else:
            right = jnp.concatenate([perm_tile(2 * q), perm_tile(2 * q + 1)], axis=1)
        left = jnp.concatenate([hilo[i] for i in range(tiles)], axis=1)
        o = jnp.dot(left, right, preferred_element_type=jnp.float32)
        out_ref[:, pl.ds(pl.multiple_of(q * WIN, WIN), WIN)] = o[:rows] + o[rows:]
        return carry

    lax.fori_loop(0, tiles, order, 0)

    for k in range(nk):
        for d in range(nz):
            below = block(z - d, y, core)
            above = block(z + d, y, core)

            @pl.when(z >= d)
            def _():
                pl.when(has_up)(lambda: copy_of(k, below, UP).wait_send())
                if ny == 2:
                    copy_of(k, below, ACROSS).wait_send()

            @pl.when(z + d < nz)
            def _():
                pl.when(has_down)(lambda: copy_of(k, above, DOWN).wait_send())
                if ny == 2 and d > 0:
                    copy_of(k, above, ACROSS).wait_send()
        for r in range(nb // 2):
            copy_of(k, r * 2 + core, SIB).wait_send()


def per_device(spectra, block_order, offsets):
    rows, bins = spectra.shape
    feats = bins // TAPS
    offs = offsets.shape[0]
    nrow, ncol = lax.axis_size("row"), lax.axis_size("col")
    nb = nrow * ncol
    total = nb * rows
    ny = 2 if nrow % 2 == 0 else 1
    nz = nrow // ny
    nk = (feats // LANE - 3 + 1) // 2 + 1
    keep_perm = total <= 2048
    cfg = (nz, ny, nb, rows, feats, offs, keep_perm)
    bf, f32 = jnp.bfloat16, jnp.float32
    any_space = pl.BlockSpec(memory_space=pl.ANY)
    vmem = pl.BlockSpec(memory_space=pltpu.VMEM)
    return pl.pallas_call(
        functools.partial(kernel, cfg),
        out_shape=jax.ShapeDtypeStruct((rows, total), f32),
        in_specs=[pl.BlockSpec(memory_space=pltpu.SMEM), any_space, vmem, vmem],
        out_specs=vmem,
        scratch_shapes=[
            pltpu.VMEM((feats // LANE, rows, TAPS * LANE), bf),
            pltpu.VMEM((feats // LANE, rows, LANE), f32),
            pltpu.VMEM((feats // LANE, nb, rows, LANE), bf),
            pltpu.VMEM((rows, feats + 2 * LANE), f32),
            pltpu.VMEM((offs * rows, WIN), bf),
            pltpu.VMEM((total // WIN, offs * rows, WIN), f32),
            pltpu.VMEM((nb, total, LANE) if keep_perm else (1, 16, LANE), bf),
            pltpu.VMEM((rows, total), bf),
            pltpu.VMEM((total // WIN, 2 * rows, WIN), bf),
            pltpu.SemaphoreType.DMA((feats // LANE,)),
            pltpu.SemaphoreType.DMA((nk, 4, nb)),
            pltpu.SemaphoreType.DMA((nk, nb)),
        ],
        compiler_params=pltpu.CompilerParams(
            collective_id=0, has_side_effects=True, vmem_limit_bytes=60 * 1024 * 1024),
    )(offsets, spectra, jnp.asarray(decimation_weights()), block_order.reshape(nb, rows))


def solution(mesh):
    in_specs = (P(("groups", "row", "col"), None), P("groups"), P())
    out_specs = P(("groups", "row", "col"), None)
    return jax.shard_map(
        per_device, mesh=mesh, in_specs=in_specs, out_specs=out_specs, check_vma=False
    )
```

```python
import functools
import math

import jax
import jax.numpy as jnp
import ml_dtypes
import numpy as np
from jax import lax
from jax.experimental import pallas as pl
from jax.experimental.pallas import tpu as pltpu
from jax.sharding import PartitionSpec as P

TAPS = 16
LANE = 128
WIN = 256
GROUP = 17
MESH = pl.DeviceIdType.MESH
UP, DOWN, ACROSS, SIB = range(4)


def decimation_weights():
    steps = np.arange(TAPS, dtype=np.float64)
    taps = (0.5 - 0.5 * np.cos(2.0 * math.pi * (steps + 0.5) / TAPS)).astype(ml_dtypes.bfloat16)
    full = np.kron(np.eye(LANE), taps.astype(np.float64)[:, None])
    return full.astype(ml_dtypes.bfloat16)


def kernel(cfg, off_ref, spec_ref, w_ref, bo_ref, out_ref,
           raw, coarse, buf, mine, stack, acc, pick,
           in_sem, send_sem, recv_sem):
    nz, ny, nb, rows, feats, offs = cfg
    chunks = [(0, 3)] + [(t, min(2, feats // LANE - t)) for t in range(3, feats // LANE, 2)]
    nk = len(chunks)
    total = nb * rows
    tiles = total // WIN
    bins_part = TAPS * LANE

    row = lax.axis_index("row")
    core = lax.axis_index("col")
    z = row // ny
    y = row % ny
    me = row * 2 + core

    def block(zz, yy, cc):
        return (zz * ny + yy) * 2 + cc

    def target(way):
        if way == UP:
            return {"row": row + ny, "col": core}
        if way == DOWN:
            return {"row": row - ny, "col": core}
        if way == ACROSS:
            return {"row": z * ny + (1 - y), "col": core}
        return {"row": row, "col": 1 - core}

    def copy_of(k, blk, way):
        first, count = chunks[k]
        ref = buf.at[pl.ds(first, count), blk]
        return pltpu.make_async_remote_copy(
            src_ref=ref, dst_ref=ref,
            send_sem=send_sem.at[k, way, blk], recv_sem=recv_sem.at[k, blk],
            device_id=target(way), device_id_type=MESH)

    def arrived(k, blk):
        copy_of(k, blk, SIB).wait_recv()

    has_up = z < nz - 1
    has_down = z > 0

    loads = []
    for g in range(feats // LANE):
        load = pltpu.make_async_copy(
            spec_ref.at[:, pl.ds(g * bins_part, bins_part)], raw.at[g], in_sem.at[g])
        load.start()
        loads.append(load)

    barrier = pltpu.get_barrier_semaphore()

    def greet(way):
        pl.semaphore_signal(barrier, inc=1, device_id=target(way), device_id_type=MESH)

    greet(SIB)
    if ny == 2:
        greet(ACROSS)
    pl.when(has_up)(lambda: greet(UP))
    pl.when(has_down)(lambda: greet(DOWN))

    square = jnp.zeros((rows, 1), jnp.float32)
    pair = 2
    for g in range(0, feats // LANE, pair):
        for h in range(pair):
            loads[g + h].wait()
        x = jnp.concatenate([raw[g + h] for h in range(pair)], axis=0)
        c = jnp.dot(x, w_ref[...], preferred_element_type=jnp.float32)
        for h in range(pair):
            part = c[h * rows:(h + 1) * rows]
            coarse[g + h] = part
            square += jnp.sum(part * part, axis=1, keepdims=True)
    scale = lax.rsqrt(square * (1.0 / feats) + 1e-06) * (1.0 / math.sqrt(feats))
    for g in range(feats // LANE):
        buf[g, me] = (coarse[g] * scale).astype(jnp.bfloat16)

    pl.semaphore_wait(barrier, 1 + (1 if ny == 2 else 0)
                      + jnp.where(has_up, 1, 0) + jnp.where(has_down, 1, 0))

    def send_own(k):
        pl.when(has_up)(lambda: copy_of(k, me, UP).start())
        pl.when(has_down)(lambda: copy_of(k, me, DOWN).start())
        if ny == 2:
            copy_of(k, me, ACROSS).start()
        copy_of(k, me, SIB).start()

    def onward(k, t):
        @pl.when(z >= t)
        def _():
            blk = block(z - t, y, core)
            arrived(k, blk)
            pl.when(has_up)(lambda: copy_of(k, blk, UP).start())
            if ny == 2:
                copy_of(k, blk, ACROSS).start()
            copy_of(k, blk, SIB).start()

        @pl.when(z + t < nz)
        def _():
            blk = block(z + t, y, core)
            arrived(k, blk)
            pl.when(has_down)(lambda: copy_of(k, blk, DOWN).start())
            if ny == 2:
                copy_of(k, blk, ACROSS).start()
            copy_of(k, blk, SIB).start()

    def share(k, d):
        def across(blk):
            arrived(k, blk)
            copy_of(k, blk, SIB).start()

        pl.when(z >= d)(lambda: across(block(z - d, 1 - y, core)))
        if d > 0:
            pl.when(z + d < nz)(lambda: across(block(z + d, 1 - y, core)))

    def finish(k):
        for r in range(nb // 2):
            arrived(k, r * 2 + (1 - core))

    events = []
    for k in range(nk):
        events.append((2 * k - 0.5, functools.partial(send_own, k)))
        for t in range(1, nz):
            events.append((2 * k + t, functools.partial(onward, k, t)))
        for d in range(nz if ny == 2 else 0):
            events.append((2 * k + d + 1.6, functools.partial(share, k, d)))
        events.append((2 * k + nz + 1, functools.partial(finish, k)))
    events.sort(key=lambda e: e[0])

    def due(k):
        low = 2 * (k - 1) + nz + 1 if k > 0 else -1
        high = 2 * k + nz + 1
        return [run for key, run in events if low < key <= high]

    first_due = due(0)
    first_due[0]()

    mine_pos = jnp.transpose(
        jnp.broadcast_to(bo_ref[pl.ds(me, 1), :].astype(jnp.float32), (LANE, LANE)))
    lane_ids = lax.broadcasted_iota(jnp.int32, (rows, LANE), 1).astype(jnp.float32)
    for b in range(nb):
        pick[:, b * LANE:(b + 1) * LANE] = jnp.where(
            mine_pos == lane_ids + float(b * LANE), 1.0, 0.0).astype(jnp.bfloat16)
    mine[:, :LANE] = jnp.zeros((rows, LANE), jnp.float32)
    mine[:, LANE + feats:] = jnp.zeros((rows, LANE), jnp.float32)

    for run in first_due[1:]:
        run()

    def window(k):
        first, count = chunks[k]
        got = jnp.concatenate(
            [buf[first + i].reshape(total, LANE) for i in range(count)], axis=1)
        mine[:, LANE * (1 + first):LANE * (1 + first + count)] = jnp.dot(
            pick[...], got, preferred_element_type=jnp.float32)
        span = mine[:, WIN * k:WIN * (k + 2)]
        for d in range(offs):
            shift = off_ref[d]
            shift = jnp.where(shift < 0, shift + 2 * WIN, shift)
            moved = pltpu.roll(span, shift, 1)
            stack[d * rows:(d + 1) * rows, :] = moved[:, LANE:LANE + WIN].astype(jnp.bfloat16)

        last = k == nk - 1
        todo = [] if last else due(k + 1)

        def tile(i, carry):
            right = jnp.concatenate(
                [buf[2 * k + h, pl.ds(2 * i, 2)].reshape(WIN, LANE) for h in range(2)], axis=1)
            best = None
            for d0 in range(0, offs, GROUP):
                d1 = min(d0 + GROUP, offs)
                s = lax.dot_general(stack[d0 * rows:d1 * rows, :], right, (((1,), (1,)), ((), ())),
                                    preferred_element_type=jnp.float32)
                if k == 0:
                    acc[i, d0 * rows:d1 * rows, :] = s
                elif not last:
                    acc[i, d0 * rows:d1 * rows, :] += s
                else:
                    s = acc[i, d0 * rows:d1 * rows, :] + s
                    for d in range(d1 - d0):
                        v = s[d * rows:(d + 1) * rows]
                        best = v if best is None else jnp.maximum(best, v)
            if last:
                out_ref[pl.ds(pl.multiple_of(i * WIN, WIN), WIN), :] = jnp.transpose(best)
            for slot in range(tiles):
                now = [run for j, run in enumerate(todo) if j * tiles // len(todo) == slot]
                if now:
                    @pl.when(i == slot)
                    def _():
                        for run in now:
                            run()
            return carry

        lax.fori_loop(0, tiles, tile, 0)

    for k in range(nk):
        window(k)

    for k in range(nk):
        for d in range(nz):
            below = block(z - d, y, core)
            above = block(z + d, y, core)

            @pl.when(z >= d)
            def _():
                pl.when(has_up)(lambda: copy_of(k, below, UP).wait_send())
                if ny == 2:
                    copy_of(k, below, ACROSS).wait_send()

            @pl.when(z + d < nz)
            def _():
                pl.when(has_down)(lambda: copy_of(k, above, DOWN).wait_send())
                if ny == 2 and d > 0:
                    copy_of(k, above, ACROSS).wait_send()
        for r in range(nb // 2):
            copy_of(k, r * 2 + core, SIB).wait_send()


def order_kernel(bo_ref, scores_ref, out_ref, gathered):
    total = scores_ref.shape[0]
    unroll = 16

    def some(g, carry):
        base = pl.multiple_of(g * unroll, unroll)
        for h in range(unroll):
            gathered[pl.ds(base + h, 1), :] = scores_ref[pl.ds(bo_ref[base + h], 1), :]
        return carry

    for t in range(total // LANE):
        lax.fori_loop(t * LANE // unroll, (t + 1) * LANE // unroll, some, 0)
        out_ref[:, t * LANE:(t + 1) * LANE] = jnp.transpose(gathered[t * LANE:(t + 1) * LANE, :])


def per_device(spectra, block_order, offsets):
    rows, bins = spectra.shape
    feats = bins // TAPS
    offs = offsets.shape[0]
    nrow, ncol = lax.axis_size("row"), lax.axis_size("col")
    nb = nrow * ncol
    total = nb * rows
    ny = 2 if nrow % 2 == 0 else 1
    nz = nrow // ny
    nk = (feats // LANE - 3 + 1) // 2 + 1
    cfg = (nz, ny, nb, rows, feats, offs)
    bf, f32 = jnp.bfloat16, jnp.float32
    any_space = pl.BlockSpec(memory_space=pl.ANY)
    vmem = pl.BlockSpec(memory_space=pltpu.VMEM)
    scores = pl.pallas_call(
        functools.partial(kernel, cfg),
        out_shape=jax.ShapeDtypeStruct((total, rows), f32),
        in_specs=[pl.BlockSpec(memory_space=pltpu.SMEM), any_space, vmem, vmem],
        out_specs=vmem,
        scratch_shapes=[
            pltpu.VMEM((feats // LANE, rows, TAPS * LANE), bf),
            pltpu.VMEM((feats // LANE, rows, LANE), f32),
            pltpu.VMEM((feats // LANE, nb, rows, LANE), bf),
            pltpu.VMEM((rows, feats + 2 * LANE), f32),
            pltpu.VMEM((offs * rows, WIN), bf),
            pltpu.VMEM((total // WIN, offs * rows, WIN), f32),
            pltpu.VMEM((rows, total), bf),
            pltpu.SemaphoreType.DMA((feats // LANE,)),
            pltpu.SemaphoreType.DMA((nk, 4, nb)),
            pltpu.SemaphoreType.DMA((nk, nb)),
        ],
        compiler_params=pltpu.CompilerParams(
            collective_id=0, has_side_effects=True, vmem_limit_bytes=60 * 1024 * 1024),
    )(offsets, spectra, jnp.asarray(decimation_weights()), block_order.reshape(nb, rows))
    return pl.pallas_call(
        order_kernel,
        out_shape=jax.ShapeDtypeStruct((rows, total), f32),
        in_specs=[pl.BlockSpec(memory_space=pltpu.SMEM), vmem],
        out_specs=vmem,
        scratch_shapes=[pltpu.VMEM((total, rows), f32)],
        compiler_params=pltpu.CompilerParams(vmem_limit_bytes=16 * 1024 * 1024),
    )(block_order, scores)


def solution(mesh):
    in_specs = (P(("groups", "row", "col"), None), P("groups"), P())
    out_specs = P(("groups", "row", "col"), None)
    return jax.shard_map(
        per_device, mesh=mesh, in_specs=in_specs, out_specs=out_specs, check_vma=False
    )
```

```python
import functools
import math

import jax
import jax.numpy as jnp
import ml_dtypes
import numpy as np
from jax import lax
from jax.experimental import pallas as pl
from jax.experimental.pallas import tpu as pltpu
from jax.sharding import PartitionSpec as P

TAPS = 16
LANE = 128
WIN = 256
GROUP = 2
TW = 1024
MESH = pl.DeviceIdType.MESH
UP, DOWN, ACROSS, SIB = range(4)


def decimation_weights():
    steps = np.arange(TAPS, dtype=np.float64)
    taps = (0.5 - 0.5 * np.cos(2.0 * math.pi * (steps + 0.5) / TAPS)).astype(ml_dtypes.bfloat16)
    full = np.kron(np.eye(LANE), taps.astype(np.float64)[:, None])
    return full.astype(ml_dtypes.bfloat16)


def kernel(cfg, off_ref, spec_ref, w_ref, bo_ref, out_ref,
           raw, coarse, buf, mine, stack, acc, pick,
           in_sem, send_sem, recv_sem):
    nz, ny, nb, rows, feats, offs = cfg
    chunks = [(0, 3)] + [(t, min(2, feats // LANE - t)) for t in range(3, feats // LANE, 2)]
    nk = len(chunks)
    total = nb * rows
    tiles = total // TW
    bins_part = TAPS * LANE

    row = lax.axis_index("row")
    core = lax.axis_index("col")
    z = row // ny
    y = row % ny
    me = row * 2 + core

    def block(zz, yy, cc):
        return (zz * ny + yy) * 2 + cc

    def target(way):
        if way == UP:
            return {"row": row + ny, "col": core}
        if way == DOWN:
            return {"row": row - ny, "col": core}
        if way == ACROSS:
            return {"row": z * ny + (1 - y), "col": core}
        return {"row": row, "col": 1 - core}

    def copy_of(k, blk, way):
        first, count = chunks[k]
        ref = buf.at[pl.ds(first, count), blk]
        return pltpu.make_async_remote_copy(
            src_ref=ref, dst_ref=ref,
            send_sem=send_sem.at[k, way, blk], recv_sem=recv_sem.at[k, blk],
            device_id=target(way), device_id_type=MESH)

    def arrived(k, blk):
        copy_of(k, blk, SIB).wait_recv()

    has_up = z < nz - 1
    has_down = z > 0

    loads = []
    for g in range(feats // LANE):
        load = pltpu.make_async_copy(
            spec_ref.at[:, pl.ds(g * bins_part, bins_part)], raw.at[g], in_sem.at[g])
        load.start()
        loads.append(load)

    barrier = pltpu.get_barrier_semaphore()

    def greet(way):
        pl.semaphore_signal(barrier, inc=1, device_id=target(way), device_id_type=MESH)

    greet(SIB)
    if ny == 2:
        greet(ACROSS)
    pl.when(has_up)(lambda: greet(UP))
    pl.when(has_down)(lambda: greet(DOWN))

    square = jnp.zeros((rows, 1), jnp.float32)
    pair = 2
    for g in range(0, feats // LANE, pair):
        for h in range(pair):
            loads[g + h].wait()
        x = jnp.concatenate([raw[g + h] for h in range(pair)], axis=0)
        c = jnp.dot(x, w_ref[...], preferred_element_type=jnp.float32)
        for h in range(pair):
            part = c[h * rows:(h + 1) * rows]
            coarse[g + h] = part
            square += jnp.sum(part * part, axis=1, keepdims=True)
    scale = lax.rsqrt(square * (1.0 / feats) + 1e-06) * (1.0 / math.sqrt(feats))
    for g in range(feats // LANE):
        buf[g, me] = (coarse[g] * scale).astype(jnp.bfloat16)

    pl.semaphore_wait(barrier, 1 + (1 if ny == 2 else 0)
                      + jnp.where(has_up, 1, 0) + jnp.where(has_down, 1, 0))

    def send_own(k):
        pl.when(has_up)(lambda: copy_of(k, me, UP).start())
        pl.when(has_down)(lambda: copy_of(k, me, DOWN).start())
        if ny == 2:
            copy_of(k, me, ACROSS).start()
        copy_of(k, me, SIB).start()

    def onward(k, t):
        @pl.when(z >= t)
        def _():
            blk = block(z - t, y, core)
            arrived(k, blk)
            pl.when(has_up)(lambda: copy_of(k, blk, UP).start())
            if ny == 2:
                copy_of(k, blk, ACROSS).start()
            copy_of(k, blk, SIB).start()

        @pl.when(z + t < nz)
        def _():
            blk = block(z + t, y, core)
            arrived(k, blk)
            pl.when(has_down)(lambda: copy_of(k, blk, DOWN).start())
            if ny == 2:
                copy_of(k, blk, ACROSS).start()
            copy_of(k, blk, SIB).start()

    def share(k, d):
        def across(blk):
            arrived(k, blk)
            copy_of(k, blk, SIB).start()

        pl.when(z >= d)(lambda: across(block(z - d, 1 - y, core)))
        if d > 0:
            pl.when(z + d < nz)(lambda: across(block(z + d, 1 - y, core)))

    def finish(k):
        for r in range(nb // 2):
            arrived(k, r * 2 + (1 - core))

    events = []
    for k in range(nk):
        events.append((2 * k - 0.5, functools.partial(send_own, k)))
        for t in range(1, nz):
            events.append((2 * k + t, functools.partial(onward, k, t)))
        for d in range(nz if ny == 2 else 0):
            events.append((2 * k + d + 1.6, functools.partial(share, k, d)))
        events.append((2 * k + nz + 1.1, functools.partial(finish, k)))
    events.sort(key=lambda e: e[0])

    def due(k):
        low = 2 * (k - 1) + nz + 1.1 if k > 0 else -10
        high = 2 * k + nz + 1.1
        return [run for key, run in events if low < key <= high]

    first_due = due(0)
    first_due[0]()

    mine_pos = jnp.transpose(
        jnp.broadcast_to(bo_ref[pl.ds(me, 1), :].astype(jnp.float32), (LANE, LANE)))
    lane_ids = lax.broadcasted_iota(jnp.int32, (rows, LANE), 1).astype(jnp.float32)
    for b in range(nb):
        pick[:, b * LANE:(b + 1) * LANE] = jnp.where(
            mine_pos == lane_ids + float(b * LANE), 1.0, 0.0).astype(jnp.bfloat16)
    mine[:, :LANE] = jnp.zeros((rows, LANE), jnp.float32)
    mine[:, LANE + feats:] = jnp.zeros((rows, LANE), jnp.float32)

    for run in first_due[1:]:
        run()

    def window(k):
        first, count = chunks[k]
        got = jnp.concatenate(
            [buf[first + i].reshape(total, LANE) for i in range(count)], axis=1)
        mine[:, LANE * (1 + first):LANE * (1 + first + count)] = jnp.dot(
            pick[...], got, preferred_element_type=jnp.float32)
        span = mine[:, WIN * k:WIN * (k + 2)]
        for d in range(offs):
            shift = off_ref[d]
            shift = jnp.where(shift < 0, shift + 2 * WIN, shift)
            moved = pltpu.roll(span, shift, 1)
            stack[d * rows:(d + 1) * rows, :] = moved[:, LANE:LANE + WIN].astype(jnp.bfloat16)

        last = k == nk - 1
        todo = [] if last else due(k + 1)

        def tile(i, carry):
            right = jnp.concatenate(
                [buf[2 * k + h, pl.ds(TW // LANE * i, TW // LANE)].reshape(TW, LANE) for h in range(2)], axis=1)
            best = None
            for d0 in range(0, offs, GROUP):
                d1 = min(d0 + GROUP, offs)
                s = lax.dot_general(stack[d0 * rows:d1 * rows, :], right, (((1,), (1,)), ((), ())),
                                    preferred_element_type=jnp.float32)
                if k == 0:
                    acc[i, d0 * rows:d1 * rows, :] = s
                elif not last:
                    acc[i, d0 * rows:d1 * rows, :] += s
                else:
                    s = acc[i, d0 * rows:d1 * rows, :] + s
                    for d in range(d1 - d0):
                        v = s[d * rows:(d + 1) * rows]
                        best = v if best is None else jnp.maximum(best, v)
            if last:
                out_ref[pl.ds(pl.multiple_of(i * TW, TW), TW), :] = jnp.transpose(best)
            for slot in range(tiles):
                now = [run for j, run in enumerate(todo) if j * tiles // len(todo) == slot]
                if now:
                    @pl.when(i == slot)
                    def _():
                        for run in now:
                            run()
            return carry

        lax.fori_loop(0, tiles, tile, 0)

    for k in range(nk):
        window(k)

    for k in range(nk):
        for d in range(nz):
            below = block(z - d, y, core)
            above = block(z + d, y, core)

            @pl.when(z >= d)
            def _():
                pl.when(has_up)(lambda: copy_of(k, below, UP).wait_send())
                if ny == 2:
                    copy_of(k, below, ACROSS).wait_send()

            @pl.when(z + d < nz)
            def _():
                pl.when(has_down)(lambda: copy_of(k, above, DOWN).wait_send())
                if ny == 2 and d > 0:
                    copy_of(k, above, ACROSS).wait_send()
        for r in range(nb // 2):
            copy_of(k, r * 2 + core, SIB).wait_send()


def order_kernel(bo_ref, scores_ref, out_ref, gathered):
    total = scores_ref.shape[0]
    unroll = 16

    def some(g, carry):
        base = pl.multiple_of(g * unroll, unroll)
        for h in range(unroll):
            gathered[pl.ds(base + h, 1), :] = scores_ref[pl.ds(bo_ref[base + h], 1), :]
        return carry

    for t in range(total // LANE):
        lax.fori_loop(t * LANE // unroll, (t + 1) * LANE // unroll, some, 0)
        out_ref[:, t * LANE:(t + 1) * LANE] = jnp.transpose(gathered[t * LANE:(t + 1) * LANE, :])


def per_device(spectra, block_order, offsets):
    rows, bins = spectra.shape
    feats = bins // TAPS
    offs = offsets.shape[0]
    nrow, ncol = lax.axis_size("row"), lax.axis_size("col")
    nb = nrow * ncol
    total = nb * rows
    ny = 2 if nrow % 2 == 0 else 1
    nz = nrow // ny
    nk = (feats // LANE - 3 + 1) // 2 + 1
    cfg = (nz, ny, nb, rows, feats, offs)
    bf, f32 = jnp.bfloat16, jnp.float32
    any_space = pl.BlockSpec(memory_space=pl.ANY)
    vmem = pl.BlockSpec(memory_space=pltpu.VMEM)
    scores = pl.pallas_call(
        functools.partial(kernel, cfg),
        out_shape=jax.ShapeDtypeStruct((total, rows), f32),
        in_specs=[pl.BlockSpec(memory_space=pltpu.SMEM), any_space, vmem, vmem],
        out_specs=vmem,
        scratch_shapes=[
            pltpu.VMEM((feats // LANE, rows, TAPS * LANE), bf),
            pltpu.VMEM((feats // LANE, rows, LANE), f32),
            pltpu.VMEM((feats // LANE, nb, rows, LANE), bf),
            pltpu.VMEM((rows, feats + 2 * LANE), f32),
            pltpu.VMEM((offs * rows, WIN), bf),
            pltpu.VMEM((total // TW, offs * rows, TW), f32),
            pltpu.VMEM((rows, total), bf),
            pltpu.SemaphoreType.DMA((feats // LANE,)),
            pltpu.SemaphoreType.DMA((nk, 4, nb)),
            pltpu.SemaphoreType.DMA((nk, nb)),
        ],
        compiler_params=pltpu.CompilerParams(
            collective_id=0, has_side_effects=True, vmem_limit_bytes=60 * 1024 * 1024),
    )(offsets, spectra, jnp.asarray(decimation_weights()), block_order.reshape(nb, rows))
    return pl.pallas_call(
        order_kernel,
        out_shape=jax.ShapeDtypeStruct((rows, total), f32),
        in_specs=[pl.BlockSpec(memory_space=pltpu.SMEM), vmem],
        out_specs=vmem,
        scratch_shapes=[pltpu.VMEM((total, rows), f32)],
        compiler_params=pltpu.CompilerParams(vmem_limit_bytes=16 * 1024 * 1024),
    )(block_order, scores)


def solution(mesh):
    in_specs = (P(("groups", "row", "col"), None), P("groups"), P())
    out_specs = P(("groups", "row", "col"), None)
    return jax.shard_map(
        per_device, mesh=mesh, in_specs=in_specs, out_specs=out_specs, check_vma=False
    )
```
